32 devices in a mesh: role: 2 (over y), tile: 16 (over z, x, core).
Axes of the slice: x: 2, y: 2, z: 4, core: 2. Of those that a mesh axis runs over, the one named last changes fastest.
Arguments:
- fields_pair: float32 [2, 512, 16384], P('role', None, 'tile'), may hold values from 0 to 1
- velocity: float32 [16384], P('tile'), may hold values from -0.5 to 0.5
- growth: float32 [16384], P('tile'), may hold values from 0.05 to 0.5
- features: bfloat16 [512, 1024], replicated, may hold values from -6 to 6
- assignment: int32 [512], replicated, may hold values from 0 to 511, each once
- out_pair: float32 [2, 1024, 16384], P('role', None, 'tile'), may hold values from -0.1875 to 0.1875
- hidden_pair: float32 [2, 5, 1024, 1024], P('role', None, 'tile'), may hold values from -0.1875 to 0.1875
Outputs:
- fields_next: float32 [2, 512, 16384], P('role', None, 'tile')
- out_next: float32 [2, 1024, 16384], P('role', None, 'tile')
- hidden_next: float32 [2, 5, 1024, 1024], P('role', None, 'tile')
The draws below stay inside these ranges and needn't reach their ends.
Inputs may be any that keep to these rules, and one draw needn't show every extreme that they name: `assignment`: a permutation of the 512 members.
All inputs are finite; a program needn't handle non-finite values.
Results may differ from the reference program's by a relative error of at most 0.0022.
The reference program's roundings to bfloat16 on the way (of `residual`) count: a program that leaves them out, or rounds other values in their place, can miss the bound.
Values may be sent and summed in bfloat16 or wider, within the bound.
A program may use at most 192 MiB of HBM per device.

```python
import math
import jax
import jax.numpy as jnp

BATCH = 512
HID = 1024
LAYERS = 5
SLAB = 16384


def block_levels(stream_key, shape, split, low, high):
    def one(dim, parts):
        steps = jax.random.uniform(jax.random.fold_in(jax.random.fold_in(stream_key, 6), dim), (parts,), jnp.float32, low / len(split), high / len(split))
        return jnp.repeat(jnp.exp(steps), shape[dim] // parts).reshape((-1,) + (1,) * (len(shape) - dim - 1))

    loudness = one(*split[0])
    for cut in split[1:]:
        loudness = loudness * one(*cut)
    return loudness


def bell_draw(own_key, dims, width, bound, split=(), kind=jnp.bfloat16):
    drawn = width * jax.random.normal(own_key, dims, jnp.float32)
    if split:
        drawn = drawn * block_levels(own_key, dims, split, -0.22, 0.18)
    return jnp.clip(drawn, -bound, bound).astype(kind)


def setup_inputs(seed: int = 0) -> dict:
    streams_of = jax.random.split(jax.random.key(seed), 8)
    return {
        "fields_pair": jnp.clip(1.0 * jax.random.uniform(streams_of[0], (2, BATCH, SLAB), jnp.float32) ** block_levels(streams_of[0], (2, BATCH, SLAB), ((0, 2), (2, 16)), -0.2, 0.2), 0.0, 1.0),
        "velocity": jnp.clip(jax.random.uniform(streams_of[1], (SLAB,), jnp.float32, -0.5, 0.5) * block_levels(streams_of[1], (SLAB,), ((0, 16),), -0.4, 0.0), -0.5, 0.5),
        "growth": jnp.clip(jnp.exp(math.log(0.5) - 2.3025851 * jax.random.uniform(streams_of[2], (SLAB,), jnp.float32) ** block_levels(streams_of[2], (SLAB,), ((0, 16),), -0.2, 0.2)), 0.05, 0.5),
        "features": bell_draw(streams_of[3], (BATCH, HID), 1.0, 6.0),
        "assignment": jax.random.permutation(streams_of[4], BATCH).astype(jnp.int32),
        "out_pair": bell_draw(streams_of[5], (2, HID, SLAB), HID ** -0.5, 0.1875, ((0, 2), (2, 16)), jnp.float32),
        "hidden_pair": bell_draw(streams_of[6], (2, LAYERS, HID, HID), HID ** -0.5, 0.1875, ((0, 2), (2, 16)), jnp.float32),
    }


def silu_slope(values):
    logistic = jax.nn.sigmoid(values)
    return logistic * (1.0 + values * (1.0 - logistic))


def reference(fields_pair, velocity, growth, features, assignment, out_pair, hidden_pair):
    current = fields_pair[0]
    target = fields_pair[1]
    forward_cell = jnp.roll(current, -1, axis=1)
    outflow = jnp.maximum(velocity, 0.0) * current + jnp.minimum(velocity, 0.0) * forward_cell
    carried = current - outflow + jnp.roll(outflow, 1, axis=1)
    advanced = carried + growth * carried * (1.0 - carried)
    next_batch = jnp.take(advanced, assignment, axis=0)
    weights = hidden_pair[1]
    momenta = hidden_pair[0]
    inputs = []
    summed_list = []
    activation = features
    for layer_index in range(LAYERS):
        inputs.append(activation)
        summed = jnp.dot(activation, weights[layer_index].astype(jnp.bfloat16), preferred_element_type=jnp.float32)
        summed_list.append(summed)
        activation = jax.nn.silu(summed).astype(jnp.bfloat16)
    out_narrow = out_pair[1].astype(jnp.bfloat16)
    predicted = jnp.dot(activation, out_narrow, preferred_element_type=jnp.float32)
    residual = ((predicted - target) / BATCH).astype(jnp.bfloat16)
    grad_out = jnp.dot(activation.T, residual, preferred_element_type=jnp.float32)
    upstream = jnp.dot(residual, out_narrow.T, preferred_element_type=jnp.float32)
    gradients = []
    for layer_index in reversed(range(LAYERS)):
        slope = (upstream * silu_slope(summed_list[layer_index])).astype(jnp.bfloat16)
        gradients.append(jnp.dot(inputs[layer_index].T, slope, preferred_element_type=jnp.float32))
        if layer_index > 0:
            upstream = jnp.dot(slope, weights[layer_index].astype(jnp.bfloat16).T, preferred_element_type=jnp.float32)
    grad_hidden = jnp.stack(gradients[::-1])
    momentum_out = 0.9 * out_pair[0] + grad_out
    weight_out = out_pair[1] - 0.1 * momentum_out
    momentum_hidden = 0.9 * momenta + grad_hidden
    weight_hidden = weights - 0.1 * momentum_hidden
    return (jnp.stack([advanced, next_batch]), jnp.stack([momentum_out, weight_out]), jnp.stack([momentum_hidden, weight_hidden]))
```

```python
import jax
import jax.numpy as jnp
from jax import lax
from jax.sharding import PartitionSpec as P

momentum_decay = 0.9
step_size = 0.1


def extended(value, axis, dim, width):
    count, length = (lax.axis_size(axis), value.shape[dim])
    up = [(i, (i + 1) % count) for i in range(count)]
    down = [(j, i) for i, j in up]
    last = lax.slice_in_dim(value, length - width, length, axis=dim)
    leading = lax.slice_in_dim(value, 0, width, axis=dim)
    before = lax.ppermute(last, axis, up)
    after = lax.ppermute(leading, axis, down)
    return jnp.concatenate([before, value, after], axis=dim)


def silu_slope(values):
    logistic = jax.nn.sigmoid(values)
    return logistic * (1.0 + values * (1.0 - logistic))


def advance(padded, growth):
    states = padded[:-1]
    velocity_row = padded[-1]
    outflow = (
        jnp.maximum(velocity_row[:-1], 0.0) * states[:, :-1]
        + jnp.minimum(velocity_row[:-1], 0.0) * states[:, 1:]
    )
    carried = states[:, 1:-1] - outflow[:, 1:] + outflow[:, :-1]
    return carried + growth * carried * (1.0 - carried)


def to_trainer(value):
    return lax.ppermute(value.astype(jnp.bfloat16), "role", [(0, 1)])


def to_solver(value):
    return lax.ppermute(value.astype(jnp.bfloat16), "role", [(1, 0)])


def plain_training(features, hidden_narrow, out_narrow, own_fields, own_out, own_hidden):
    layer_count, unit_rows = own_hidden.shape[:2]
    batch = own_fields.shape[0]
    first_unit = lax.axis_index("tile") * unit_rows
    momentum_out = to_trainer(own_out)
    momentum_hidden = to_trainer(own_hidden)
    full_hidden = [
        lax.all_gather(hidden_narrow[i], "tile", axis=0, tiled=True) for i in range(layer_count)
    ]
    inputs, summed_list = [], []
    activation = features
    for i in range(layer_count):
        inputs.append(activation)
        summed = jnp.dot(activation, full_hidden[i], preferred_element_type=jnp.float32)
        summed_list.append(summed)
        activation = jax.nn.silu(summed).astype(jnp.bfloat16)
    predicted = jnp.dot(activation, out_narrow, preferred_element_type=jnp.float32)
    residual = ((predicted - own_fields) / batch).astype(jnp.bfloat16)
    partial_grad = lax.dot_general(
        residual, out_narrow, (((1,), (1,)), ((), ())), preferred_element_type=jnp.float32
    )
    upstream = lax.psum(partial_grad, "tile")
    grad_out = jnp.dot(activation.T, residual, preferred_element_type=jnp.float32)
    sent_out = to_solver(grad_out)
    gradients, sent = [], []
    for i in reversed(range(layer_count)):
        slope = (upstream * silu_slope(summed_list[i])).astype(jnp.bfloat16)
        own_inputs = lax.dynamic_slice_in_dim(inputs[i], first_unit, unit_rows, 1)
        gradient = jnp.dot(own_inputs.T, slope, preferred_element_type=jnp.float32)
        gradients.append(gradient)
        sent.append(to_solver(gradient))
        if i > 0:
            upstream = lax.dot_general(
                slope, full_hidden[i], (((1,), (1,)), ((), ())), preferred_element_type=jnp.float32
            )
    solver_side = lax.axis_index("role") == 0
    other_out = jnp.where(solver_side, sent_out, momentum_out)
    other_hidden = jnp.where(solver_side, jnp.stack(sent[::-1]), momentum_hidden)
    return grad_out, jnp.stack(gradients[::-1]), other_out, other_hidden


def body(fields_pair, velocity, growth, features, assignment, out_pair, hidden_pair):
    solver_side = lax.axis_index("role") == 0
    own_fields = fields_pair[0]
    own_out = out_pair[0]
    own_hidden = hidden_pair[0]
    stacked = jnp.concatenate([own_fields, velocity[None, :]], axis=0)
    advanced = advance(extended(stacked, "tile", 1, 1), growth)
    fresh_fields = to_trainer(advanced)
    grad_out, grad_hidden, other_out, other_hidden = plain_training(
        features,
        own_hidden.astype(jnp.bfloat16),
        own_out.astype(jnp.bfloat16),
        own_fields,
        own_out,
        own_hidden,
    )
    grad_out, grad_hidden, other_out, other_hidden = (
        v.astype(jnp.float32) for v in (grad_out, grad_hidden, other_out, other_hidden)
    )
    out_next = jnp.where(
        solver_side,
        momentum_decay * own_out + other_out,
        own_out - step_size * (momentum_decay * other_out + grad_out),
    )
    hidden_next = jnp.where(
        solver_side,
        momentum_decay * own_hidden + other_hidden,
        own_hidden - step_size * (momentum_decay * other_hidden + grad_hidden),
    )
    next_batch = jnp.take(fresh_fields, assignment, axis=0).astype(jnp.float32)
    fields_next = jnp.where(solver_side, advanced, next_batch)
    return (fields_next[None], out_next[None], hidden_next[None])


def solution(mesh):
    return jax.shard_map(
        body,
        mesh=mesh,
        in_specs=(
            P("role", None, "tile"),
            P("tile"),
            P("tile"),
            P(),
            P(),
            P("role", None, "tile"),
            P("role", None, "tile", None),
        ),
        out_specs=(P("role", None, "tile"), P("role", None, "tile"), P("role", None, "tile", None)),
        check_vma=False,
    )
```

```python
import functools

import jax
import jax.numpy as jnp
from jax import lax
from jax.experimental import pallas as pl
from jax.experimental.pallas import tpu as pltpu
from jax.sharding import PartitionSpec as P

momentum_decay = 0.9
step_size = 0.1


def extended(value, axis, dim, width):
    count, length = (lax.axis_size(axis), value.shape[dim])
    up = [(i, (i + 1) % count) for i in range(count)]
    down = [(j, i) for i, j in up]
    last = lax.slice_in_dim(value, length - width, length, axis=dim)
    leading = lax.slice_in_dim(value, 0, width, axis=dim)
    before = lax.ppermute(last, axis, up)
    after = lax.ppermute(leading, axis, down)
    return jnp.concatenate([before, value, after], axis=dim)


def silu_slope(values):
    logistic = jax.nn.sigmoid(values)
    return logistic * (1.0 + values * (1.0 - logistic))


def advance(padded, growth):
    states = padded[:-1]
    velocity_row = padded[-1]
    outflow = (
        jnp.maximum(velocity_row[:-1], 0.0) * states[:, :-1]
        + jnp.minimum(velocity_row[:-1], 0.0) * states[:, 1:]
    )
    carried = states[:, 1:-1] - outflow[:, 1:] + outflow[:, :-1]
    return carried + growth * carried * (1.0 - carried)


def to_trainer(value):
    return lax.ppermute(value.astype(jnp.bfloat16), "role", [(0, 1)])


def to_solver(value):
    return lax.ppermute(value.astype(jnp.bfloat16), "role", [(1, 0)])


def plain_training(features, hidden_narrow, out_narrow, own_fields, own_out, own_hidden):
    layer_count, unit_rows = own_hidden.shape[:2]
    batch = own_fields.shape[0]
    first_unit = lax.axis_index("tile") * unit_rows
    momentum_out = to_trainer(own_out)
    momentum_hidden = to_trainer(own_hidden)
    full_hidden = [
        lax.all_gather(hidden_narrow[i], "tile", axis=0, tiled=True) for i in range(layer_count)
    ]
    inputs, summed_list = [], []
    activation = features
    for i in range(layer_count):
        inputs.append(activation)
        summed = jnp.dot(activation, full_hidden[i], preferred_element_type=jnp.float32)
        summed_list.append(summed)
        activation = jax.nn.silu(summed).astype(jnp.bfloat16)
    predicted = jnp.dot(activation, out_narrow, preferred_element_type=jnp.float32)
    residual = ((predicted - own_fields) / batch).astype(jnp.bfloat16)
    partial_grad = lax.dot_general(
        residual, out_narrow, (((1,), (1,)), ((), ())), preferred_element_type=jnp.float32
    )
    upstream = lax.psum(partial_grad, "tile")
    grad_out = jnp.dot(activation.T, residual, preferred_element_type=jnp.float32)
    sent_out = to_solver(grad_out)
    gradients, sent = [], []
    for i in reversed(range(layer_count)):
        slope = (upstream * silu_slope(summed_list[i])).astype(jnp.bfloat16)
        own_inputs = lax.dynamic_slice_in_dim(inputs[i], first_unit, unit_rows, 1)
        gradient = jnp.dot(own_inputs.T, slope, preferred_element_type=jnp.float32)
        gradients.append(gradient)
        sent.append(to_solver(gradient))
        if i > 0:
            upstream = lax.dot_general(
                slope, full_hidden[i], (((1,), (1,)), ((), ())), preferred_element_type=jnp.float32
            )
    solver_side = lax.axis_index("role") == 0
    other_out = jnp.where(solver_side, sent_out, momentum_out)
    other_hidden = jnp.where(solver_side, jnp.stack(sent[::-1]), momentum_hidden)
    return grad_out, jnp.stack(gradients[::-1]), other_out, other_hidden


LANES = 128
COLUMNS = 256


def train_kernel(
    groups,
    features_ref,
    hidden_ref,
    out_ref,
    target_ref,
    sent_out_ref,
    sent_hidden_ref,
    got_out_ref,
    got_hidden_ref,
    weights,
    inputs,
    factors,
    residual,
    partial,
    slope,
    payload,
    payload_hidden,
    gradient,
    core_sum,
    x_sum,
    z_sum,
    gather_send,
    gather_recv,
    sum_send,
    sum_recv,
    slope_send,
    slope_recv,
    role_send,
    role_recv,
    local_sem,
):
    layer_count, unit_rows, width = hidden_ref.shape
    batch = features_ref.shape[0]
    rows = partial.shape[3]
    role = lax.axis_index("role")
    tile = lax.axis_index("tile")
    core = lax.rem(tile, 2)
    x = lax.rem(tile // 2, 2)
    z = tile // 4
    solver_side = role == 0

    def device(z_at, x_at, core_at):
        return (role, z_at * 4 + x_at * 2 + core_at)

    z_places = [lax.rem(z + k, groups) for k in range(1, groups)]
    z_peers = [device(place, x, core) for place in z_places]
    x_peer = device(z, 1 - x, core)
    core_peer = device(z, x, 1 - core)
    role_peer = (1 - role, tile)

    def send(source, target, send_sem, recv_sem, peer):
        copy = pltpu.make_async_remote_copy(
            src_ref=source,
            dst_ref=target,
            send_sem=send_sem,
            recv_sem=recv_sem,
            device_id=peer,
            device_id_type=pl.DeviceIdType.MESH,
        )
        copy.start()
        return copy

    own = pltpu.make_async_copy(hidden_ref, weights.at[:, z, x, core], local_sem.at[0])
    own.start()
    barrier = pltpu.get_barrier_semaphore()
    peers = z_peers + [x_peer, core_peer, role_peer]
    for peer in peers:
        pl.semaphore_signal(barrier, inc=1, device_id=peer, device_id_type=pl.DeviceIdType.MESH)
    pl.semaphore_wait(barrier, len(peers))

    sends = []
    z_copies = []
    for i in range(layer_count):
        z_copies.append(
            [
                send(
                    hidden_ref.at[i],
                    weights.at[i, z, x, core],
                    gather_send.at[i, k],
                    gather_recv.at[i, k],
                    z_peers[k],
                )
                for k in range(groups - 1)
            ]
        )
        sends += z_copies[-1]
    own.wait()

    def columns_of(j):
        return pl.ds(pl.multiple_of(j * COLUMNS, COLUMNS), COLUMNS)

    def forward(i):
        @pl.loop(0, width // COLUMNS)
        def _(j):
            columns = columns_of(j)
            block = weights[i, :, :, :, :, columns].reshape(width, COLUMNS)
            activation = features_ref[...] if i == 0 else inputs[i - 1]
            summed = jnp.dot(activation, block, preferred_element_type=jnp.float32)
            logistic = jax.nn.sigmoid(summed)
            inputs[i, :, columns] = (summed * logistic).astype(jnp.bfloat16)
            factors[i, :, columns] = logistic * (1.0 + summed * (1.0 - logistic))

    x_copies, core_copies = [], []
    for i in range(layer_count + 2):
        if i < layer_count:
            for copy in z_copies[i]:
                copy.wait_recv()
            view = weights.at[i, :, x, core]
            x_copies.append(
                send(view, view, gather_send.at[i, groups - 1], gather_recv.at[i, groups - 1], x_peer)
            )
        if 1 <= i <= layer_count:
            x_copies[i - 1].wait_recv()
            view = weights.at[i - 1, :, :, core]
            core_copies.append(
                send(
                    view,
                    view,
                    gather_send.at[i - 1, groups],
                    gather_recv.at[i - 1, groups],
                    core_peer,
                )
            )
        if i >= 2:
            core_copies[i - 2].wait_recv()
            forward(i - 2)
    sends += x_copies + core_copies

    last = layer_count - 1

    @pl.loop(0, width // COLUMNS)
    def _(j):
        columns = columns_of(j)
        predicted = jnp.dot(inputs[last], out_ref[:, columns], preferred_element_type=jnp.float32)
        residual[:, columns] = ((predicted - target_ref[:, columns]) / batch).astype(jnp.bfloat16)

    @pl.loop(0, width // COLUMNS)
    def _(j):
        columns = columns_of(j)
        part = lax.dot_general(
            residual[...],
            out_ref[columns, :],
            (((1,), (1,)), ((), ())),
            preferred_element_type=jnp.float32,
        )
        partial[:, :, :, :, columns] = part.reshape(groups, 2, 2, rows, COLUMNS)

    core_copy = send(
        partial.at[:, :, 1 - core], core_sum, sum_send.at[0], sum_recv.at[0], core_peer
    )

    @pl.loop(0, width // COLUMNS)
    def _(j):
        columns = columns_of(j)
        grad = lax.dot_general(
            inputs[last],
            residual[:, columns],
            (((0,), (0,)), ((), ())),
            preferred_element_type=jnp.float32,
        )
        payload[:, columns] = jnp.where(solver_side, out_ref[:, columns], grad.astype(jnp.bfloat16))

    core_copy.wait_recv()
    away = partial[:, 1 - x, core] + core_sum[:, 1 - x]
    partial[:, 1 - x, core] = away
    x_copy = send(partial.at[:, 1 - x, core], x_sum, sum_send.at[1], sum_recv.at[1], x_peer)
    out_copy = send(payload, got_out_ref, role_send.at[0], role_recv.at[0], role_peer)
    out_keep = pltpu.make_async_copy(payload, sent_out_ref, local_sem.at[0])
    out_keep.start()
    partial[:, x, core] = partial[:, x, core] + core_sum[:, x]
    x_copy.wait_recv()
    partial[:, x, core] = partial[:, x, core] + x_sum[...]
    z_sums = [
        send(
            partial.at[z_places[k], x, core],
            z_sum.at[k],
            sum_send.at[2 + k],
            sum_recv.at[2 + k],
            z_peers[k],
        )
        for k in range(groups - 1)
    ]
    upstream = partial[z, x, core]
    for k in range(groups - 1):
        z_sums[k].wait_recv()
        upstream = upstream + z_sum[k]
    own_rows = pl.ds(pl.multiple_of(tile * rows, rows), rows)
    slope[z, x, core] = (upstream * factors[last, own_rows, :]).astype(jnp.bfloat16)
    view = slope.at[z, x, core]
    z_slopes = [
        send(view, view, slope_send.at[k], slope_recv.at[k], z_peers[k]) for k in range(groups - 1)
    ]
    for copy in z_slopes:
        copy.wait_recv()
    view = slope.at[:, x, core]
    x_slope = send(view, view, slope_send.at[groups - 1], slope_recv.at[groups - 1], x_peer)
    x_slope.wait_recv()
    view = slope.at[:, :, core]
    core_slope = send(view, view, slope_send.at[groups], slope_recv.at[groups], core_peer)
    core_slope.wait_recv()
    sends += [core_copy, x_copy, out_copy] + z_sums
    for copy in z_slopes + [x_slope, core_slope]:
        copy.wait_send()

    per_block = LANES // unit_rows
    first_lane = pl.multiple_of((tile // per_block) * LANES, LANES)
    unit_first = pl.multiple_of(lax.rem(tile, per_block) * unit_rows, unit_rows)
    role_copies = []
    for i in reversed(range(layer_count)):
        source = features_ref if i == 0 else inputs.at[i - 1]
        own_inputs = source[:, pl.ds(first_lane, LANES)]

        @pl.loop(0, width // COLUMNS)
        def _(j):
            columns = columns_of(j)
            gradient[:, columns] = lax.dot_general(
                own_inputs,
                slope[:, :, :, :, columns].reshape(batch, COLUMNS),
                (((0,), (0,)), ((), ())),
                preferred_element_type=jnp.float32,
            )

        mine = gradient[pl.ds(unit_first, unit_rows), :].astype(jnp.bfloat16)
        payload_hidden[i] = jnp.where(solver_side, hidden_ref[i], mine)
        if i > 0:
            whole_slope = slope[...].reshape(batch, width)

            @pl.loop(0, width // COLUMNS)
            def _(j):
                columns = columns_of(j)
                block = weights.at[i].reshape(width, width)[columns, :]
                back = lax.dot_general(
                    whole_slope,
                    block,
                    (((1,), (1,)), ((), ())),
                    preferred_element_type=jnp.float32,
                )
                residual[:, columns] = (back * factors[i - 1, :, columns]).astype(jnp.bfloat16)

        role_copies.append(
            send(
                payload_hidden.at[i],
                got_hidden_ref.at[i],
                role_send.at[1 + i],
                role_recv.at[1 + i],
                role_peer,
            )
        )
        if i > 0:
            slope[...] = residual[...].reshape(slope.shape)
    hidden_keep = pltpu.make_async_copy(payload_hidden, sent_hidden_ref, local_sem.at[1])
    hidden_keep.start()
    sends += role_copies
    out_copy.wait_recv()
    for copy in role_copies:
        copy.wait_recv()
    for copy in sends:
        copy.wait_send()
    out_keep.wait()
    hidden_keep.wait()


def fused_training(features, hidden_narrow, out_narrow, own_fields, own_out, own_hidden):
    layer_count, unit_rows, width = hidden_narrow.shape
    batch, cells = own_fields.shape
    groups = lax.axis_size("tile") // 4
    rows = batch // lax.axis_size("tile")
    narrow, wide = jnp.bfloat16, jnp.float32
    dma = pltpu.SemaphoreType.DMA
    vmem = pl.BlockSpec(memory_space=pltpu.VMEM)
    anywhere = pl.BlockSpec(memory_space=pl.ANY)
    return pl.pallas_call(
        functools.partial(train_kernel, groups),
        out_shape=(
            jax.ShapeDtypeStruct((width, cells), narrow),
            jax.ShapeDtypeStruct(hidden_narrow.shape, narrow),
            jax.ShapeDtypeStruct((width, cells), narrow),
            jax.ShapeDtypeStruct(hidden_narrow.shape, narrow),
        ),
        in_specs=[vmem] * 4,
        out_specs=[anywhere] * 4,
        scratch_shapes=[
            pltpu.VMEM((layer_count, groups, 2, 2, unit_rows, width), narrow),
            pltpu.VMEM((layer_count, batch, width), narrow),
            pltpu.VMEM((layer_count, batch, width), wide),
            pltpu.VMEM((batch, cells), narrow),
            pltpu.VMEM((groups, 2, 2, rows, width), wide),
            pltpu.VMEM((groups, 2, 2, rows, width), narrow),
            pltpu.VMEM((width, cells), narrow),
            pltpu.VMEM(hidden_narrow.shape, narrow),
            pltpu.VMEM((LANES, width), wide),
            pltpu.VMEM((groups, 2, rows, width), wide),
            pltpu.VMEM((groups, rows, width), wide),
            pltpu.VMEM((groups - 1, rows, width), wide),
            dma((layer_count, groups + 1)),
            dma((layer_count, groups + 1)),
            dma((groups + 1,)),
            dma((groups + 1,)),
            dma((groups + 1,)),
            dma((groups + 1,)),
            dma((layer_count + 1,)),
            dma((layer_count + 1,)),
            dma((2,)),
        ],
        compiler_params=pltpu.CompilerParams(
            collective_id=0, has_side_effects=True, vmem_limit_bytes=64000000
        ),
        cost_estimate=pl.CostEstimate(
            flops=60 * batch * width * width, bytes_accessed=40 * batch * width, transcendentals=0
        ),
    )(features, hidden_narrow, out_narrow, own_fields)


def training(features, hidden_narrow, out_narrow, own_fields, own_out, own_hidden):
    tiles = lax.axis_size("tile")
    fits = (
        tiles % 4 == 0
        and tiles > 4
        and (own_fields.shape[0] // tiles) % 16 == 0
        and LANES % own_hidden.shape[1] == 0
    )
    chosen = fused_training if fits else plain_training
    return chosen(features, hidden_narrow, out_narrow, own_fields, own_out, own_hidden)


def body(fields_pair, velocity, growth, features, assignment, out_pair, hidden_pair):
    solver_side = lax.axis_index("role") == 0
    own_fields = fields_pair[0]
    own_out = out_pair[0]
    own_hidden = hidden_pair[0]
    stacked = jnp.concatenate([own_fields, velocity[None, :]], axis=0)
    advanced = advance(extended(stacked, "tile", 1, 1), growth)
    fresh_fields = to_trainer(advanced)
    grad_out, grad_hidden, other_out, other_hidden = training(
        features,
        own_hidden.astype(jnp.bfloat16),
        own_out.astype(jnp.bfloat16),
        own_fields,
        own_out,
        own_hidden,
    )
    grad_out, grad_hidden, other_out, other_hidden = (
        v.astype(jnp.float32) for v in (grad_out, grad_hidden, other_out, other_hidden)
    )
    out_next = jnp.where(
        solver_side,
        momentum_decay * own_out + other_out,
        own_out - step_size * (momentum_decay * other_out + grad_out),
    )
    hidden_next = jnp.where(
        solver_side,
        momentum_decay * own_hidden + other_hidden,
        own_hidden - step_size * (momentum_decay * other_hidden + grad_hidden),
    )
    next_batch = jnp.take(fresh_fields, assignment, axis=0).astype(jnp.float32)
    fields_next = jnp.where(solver_side, advanced, next_batch)
    return (fields_next[None], out_next[None], hidden_next[None])


def solution(mesh):
    return jax.shard_map(
        body,
        mesh=mesh,
        in_specs=(
            P("role", None, "tile"),
            P("tile"),
            P("tile"),
            P(),
            P(),
            P("role", None, "tile"),
            P("role", None, "tile", None),
        ),
        out_specs=(P("role", None, "tile"), P("role", None, "tile"), P("role", None, "tile", None)),
        check_vma=False,
    )
```

```python
import functools

import jax
import jax.numpy as jnp
from jax import lax
from jax.experimental import pallas as pl
from jax.experimental.pallas import tpu as pltpu
from jax.sharding import PartitionSpec as P

momentum_decay = 0.9
step_size = 0.1


def extended(value, axis, dim, width):
    count, length = (lax.axis_size(axis), value.shape[dim])
    up = [(i, (i + 1) % count) for i in range(count)]
    down = [(j, i) for i, j in up]
    last = lax.slice_in_dim(value, length - width, length, axis=dim)
    leading = lax.slice_in_dim(value, 0, width, axis=dim)
    before = lax.ppermute(last, axis, up)
    after = lax.ppermute(leading, axis, down)
    return jnp.concatenate([before, value, after], axis=dim)


def silu_slope(values):
    logistic = jax.nn.sigmoid(values)
    return logistic * (1.0 + values * (1.0 - logistic))


def advance(padded, growth):
    states = padded[:-1]
    velocity_row = padded[-1]
    outflow = (
        jnp.maximum(velocity_row[:-1], 0.0) * states[:, :-1]
        + jnp.minimum(velocity_row[:-1], 0.0) * states[:, 1:]
    )
    carried = states[:, 1:-1] - outflow[:, 1:] + outflow[:, :-1]
    return carried + growth * carried * (1.0 - carried)


def to_trainer(value):
    return lax.ppermute(value.astype(jnp.bfloat16), "role", [(0, 1)])


def to_solver(value):
    return lax.ppermute(value.astype(jnp.bfloat16), "role", [(1, 0)])


def plain_training(features, hidden_narrow, out_narrow, own_fields, own_out, own_hidden, fields):
    layer_count, unit_rows = own_hidden.shape[:2]
    batch = own_fields.shape[0]
    first_unit = lax.axis_index("tile") * unit_rows
    momentum_out = to_trainer(own_out)
    momentum_hidden = to_trainer(own_hidden)
    full_hidden = [
        lax.all_gather(hidden_narrow[i], "tile", axis=0, tiled=True) for i in range(layer_count)
    ]
    inputs, summed_list = [], []
    activation = features
    for i in range(layer_count):
        inputs.append(activation)
        summed = jnp.dot(activation, full_hidden[i], preferred_element_type=jnp.float32)
        summed_list.append(summed)
        activation = jax.nn.silu(summed).astype(jnp.bfloat16)
    predicted = jnp.dot(activation, out_narrow, preferred_element_type=jnp.float32)
    residual = ((predicted - own_fields) / batch).astype(jnp.bfloat16)
    partial_grad = lax.dot_general(
        residual, out_narrow, (((1,), (1,)), ((), ())), preferred_element_type=jnp.float32
    )
    upstream = lax.psum(partial_grad, "tile")
    grad_out = jnp.dot(activation.T, residual, preferred_element_type=jnp.float32)
    sent_out = to_solver(grad_out)
    gradients, sent = [], []
    for i in reversed(range(layer_count)):
        slope = (upstream * silu_slope(summed_list[i])).astype(jnp.bfloat16)
        own_inputs = lax.dynamic_slice_in_dim(inputs[i], first_unit, unit_rows, 1)
        gradient = jnp.dot(own_inputs.T, slope, preferred_element_type=jnp.float32)
        gradients.append(gradient)
        sent.append(to_solver(gradient))
        if i > 0:
            upstream = lax.dot_general(
                slope, full_hidden[i], (((1,), (1,)), ((), ())), preferred_element_type=jnp.float32
            )
    solver_side = lax.axis_index("role") == 0
    other_out = jnp.where(solver_side, sent_out, momentum_out)
    other_hidden = jnp.where(solver_side, jnp.stack(sent[::-1]), momentum_hidden)
    return grad_out, jnp.stack(gradients[::-1]), other_out, other_hidden, to_trainer(fields)


LANES = 128
COLUMNS = 256


def train_kernel(
    groups,
    features_hbm,
    hidden_ref,
    out_hbm,
    target_hbm,
    fields_hbm,
    sent_out_ref,
    sent_hidden_ref,
    got_out_ref,
    got_hidden_ref,
    got_fields_ref,
    features_ref,
    out_ref,
    target_ref,
    weights,
    inputs,
    factors,
    residual,
    partial,
    slope,
    payload,
    payload_hidden,
    gradient,
    core_sum,
    x_away,
    x_sum,
    z_away,
    z_sum,
    z_send,
    z_recv,
    x_send,
    x_recv,
    core_send,
    core_recv,
    sum_send,
    sum_recv,
    slope_send,
    slope_recv,
    role_send,
    role_recv,
    local_sem,
):
    layer_count, unit_rows, width = hidden_ref.shape
    batch, cells = target_ref.shape
    rows = partial.shape[3]
    role = lax.axis_index("role")
    tile = lax.axis_index("tile")
    core = lax.rem(tile, 2)
    x = lax.rem(tile // 2, 2)
    z = tile // 4
    solver_side = role == 0

    def device(z_at, x_at, core_at):
        return (role, z_at * 4 + x_at * 2 + core_at)

    z_places = [lax.rem(z + k, groups) for k in range(1, groups)]
    z_origins = [lax.rem(z + groups - k, groups) for k in range(1, groups)]
    z_peers = [device(place, x, core) for place in z_places]
    x_peer = device(z, 1 - x, core)
    core_peer = device(z, x, 1 - core)
    role_peer = (1 - role, tile)
    sends = []

    def send(source, target, send_sem, recv_sem, peer):
        copy = pltpu.make_async_remote_copy(
            src_ref=source,
            dst_ref=target,
            send_sem=send_sem,
            recv_sem=recv_sem,
            device_id=peer,
            device_id_type=pl.DeviceIdType.MESH,
        )
        copy.start()
        sends.append(copy)
        return copy

    own = pltpu.make_async_copy(hidden_ref, weights.at[:, z, x, core], local_sem.at[0])
    own.start()
    loads = [
        pltpu.make_async_copy(features_hbm, features_ref, local_sem.at[1]),
        pltpu.make_async_copy(out_hbm, out_ref, local_sem.at[2]),
        pltpu.make_async_copy(target_hbm, target_ref, local_sem.at[3]),
    ]
    for load in loads:
        load.start()
    barrier = pltpu.get_barrier_semaphore()
    peers = z_peers + [x_peer, core_peer, role_peer]
    for peer in peers:
        pl.semaphore_signal(barrier, inc=1, device_id=peer, device_id_type=pl.DeviceIdType.MESH)
    pl.semaphore_wait(barrier, len(peers))

    x_copies = [[] for _ in range(layer_count)]

    def send_x(i, slot, source, place):
        x_copies[i].append(
            send(
                source,
                weights.at[i, place, x, core],
                x_send.at[i, slot],
                x_recv.at[i, slot],
                x_peer,
            )
        )

    z_copies = []
    for i in range(layer_count):
        z_copies.append(
            [
                send(
                    hidden_ref.at[i],
                    weights.at[i, z, x, core],
                    z_send.at[i, k],
                    z_recv.at[i, k],
                    z_peers[k],
                )
                for k in range(groups - 1)
            ]
        )
        if i < 2:
            send_x(i, 0, hidden_ref.at[i], z)
    last = layer_count - 1
    fields_copy = send(
        fields_hbm,
        got_fields_ref,
        role_send.at[0],
        role_recv.at[0],
        role_peer,
    )
    own.wait()
    for load in loads:
        load.wait()

    def columns_of(j):
        return pl.ds(pl.multiple_of(j * COLUMNS, COLUMNS), COLUMNS)

    def forward(i):
        @pl.loop(0, width // COLUMNS)
        def _(j):
            columns = columns_of(j)
            block = weights[i, :, :, :, :, columns].reshape(width, COLUMNS)
            activation = features_ref[...] if i == 0 else inputs[i - 1]
            summed = jnp.dot(activation, block, preferred_element_type=jnp.float32)
            logistic = jax.nn.sigmoid(summed)
            inputs[i, :, columns] = (summed * logistic).astype(jnp.bfloat16)
            factors[i, :, columns] = logistic * (1.0 + summed * (1.0 - logistic))

    core_copies = []
    for i in range(layer_count + 2):
        if i < layer_count:
            for k in range(groups - 1):
                z_copies[i][k].wait_recv()
                send_x(i, k + 1, weights.at[i, z_origins[k], x, core], z_origins[k])
            if i + 2 < layer_count:
                send_x(i + 2, 0, hidden_ref.at[i + 2], z)
        if 1 <= i <= layer_count:
            for copy in x_copies[i - 1]:
                copy.wait_recv()
            view = weights.at[i - 1, :, :, core]
            core_copies.append(
                send(view, view, core_send.at[i - 1], core_recv.at[i - 1], core_peer)
            )
        if i >= 2:
            core_copies[i - 2].wait_recv()
            forward(i - 2)

    role_slot = 1
    chunks = [pl.ds(j * COLUMNS, COLUMNS) for j in range(cells // COLUMNS)]
    role_copies = [fields_copy]
    for columns in chunks:
        predicted = jnp.dot(inputs[last], out_ref[:, columns], preferred_element_type=jnp.float32)
        residual[:, columns] = ((predicted - target_ref[:, columns]) / batch).astype(jnp.bfloat16)
    for columns in chunks:
        grad = lax.dot_general(
            inputs[last],
            residual[:, columns],
            (((0,), (0,)), ((), ())),
            preferred_element_type=jnp.float32,
        )
        payload[:, columns] = jnp.where(solver_side, out_ref[:, columns], grad.astype(jnp.bfloat16))
        role_copies.append(
            send(
                payload.at[:, columns],
                got_out_ref.at[:, columns],
                role_send.at[role_slot],
                role_recv.at[role_slot],
                role_peer,
            )
        )
        role_slot += 1
    out_keep = pltpu.make_async_copy(payload, sent_out_ref, local_sem.at[0])
    out_keep.start()

    parts = [pl.ds(j * COLUMNS, COLUMNS) for j in range(width // COLUMNS)]
    core_sums, x_sums, z_sums, z_slopes, x_slopes, core_slopes = [], [], [], [], [], []
    for j, columns in enumerate(parts):
        part = lax.dot_general(
            residual[...],
            out_ref[columns, :],
            (((1,), (1,)), ((), ())),
            preferred_element_type=jnp.float32,
        )
        partial[:, :, :, :, columns] = part.reshape(groups, 2, 2, rows, COLUMNS)
        core_sums.append(
            send(
                partial.at[:, :, 1 - core, :, columns],
                core_sum.at[:, :, :, columns],
                sum_send.at[j, 0],
                sum_recv.at[j, 0],
                core_peer,
            )
        )
    for j, columns in enumerate(parts):
        core_sums[j].wait_recv()
        away = partial[:, 1 - x, core, :, columns] + core_sum[:, 1 - x, :, columns]
        x_away[:, :, columns] = away.astype(jnp.bfloat16)
        x_sums.append(
            send(
                x_away.at[:, :, columns],
                x_sum.at[:, :, columns],
                sum_send.at[j, 1],
                sum_recv.at[j, 1],
                x_peer,
            )
        )
    for j, columns in enumerate(parts):
        kept = partial[:, x, core, :, columns] + core_sum[:, x, :, columns]
        x_sums[j].wait_recv()
        kept = kept + x_sum[:, :, columns].astype(jnp.float32)
        partial[:, x, core, :, columns] = kept
        z_away[:, :, columns] = kept.astype(jnp.bfloat16)
        z_sums.append(
            [
                send(
                    z_away.at[z_places[k], :, columns],
                    z_sum.at[k, :, columns],
                    sum_send.at[j, 2 + k],
                    sum_recv.at[j, 2 + k],
                    z_peers[k],
                )
                for k in range(groups - 1)
            ]
        )
    own_rows = pl.ds(pl.multiple_of(tile * rows, rows), rows)

    def send_slope(view, j, slot, peer):
        return send(view, view, slope_send.at[j, slot], slope_recv.at[j, slot], peer)

    for j, columns in enumerate(parts):
        upstream = partial[z, x, core, :, columns]
        for k in range(groups - 1):
            z_sums[j][k].wait_recv()
            upstream = upstream + z_sum[k, :, columns].astype(jnp.float32)
        slope[z, x, core, :, columns] = (upstream * factors[last, own_rows, columns]).astype(
            jnp.bfloat16
        )
        view = slope.at[z, x, core, :, columns]
        z_slopes.append([send_slope(view, j, k, z_peers[k]) for k in range(groups - 1)])
    for j, columns in enumerate(parts):
        for copy in z_slopes[j]:
            copy.wait_recv()
        view = slope.at[:, x, core, :, columns]
        x_slopes.append(send_slope(view, j, groups - 1, x_peer))
    for j, columns in enumerate(parts):
        x_slopes[j].wait_recv()
        core_slopes.append(send_slope(slope.at[:, :, core, :, columns], j, groups, core_peer))
    for copy in core_slopes:
        copy.wait_recv()
    for copies in z_slopes + [x_slopes, core_slopes]:
        for copy in copies:
            copy.wait_send()
            sends[:] = [other for other in sends if other is not copy]

    per_block = LANES // unit_rows
    first_lane = pl.multiple_of((tile // per_block) * LANES, LANES)
    unit_first = pl.multiple_of(lax.rem(tile, per_block) * unit_rows, unit_rows)
    for i in reversed(range(layer_count)):
        source = features_ref if i == 0 else inputs.at[i - 1]
        own_inputs = source[:, pl.ds(first_lane, LANES)]

        @pl.loop(0, width // COLUMNS)
        def _(j):
            columns = columns_of(j)
            gradient[:, columns] = lax.dot_general(
                own_inputs,
                slope[:, :, :, :, columns].reshape(batch, COLUMNS),
                (((0,), (0,)), ((), ())),
                preferred_element_type=jnp.float32,
            )

        mine = gradient[pl.ds(unit_first, unit_rows), :].astype(jnp.bfloat16)
        payload_hidden[i] = jnp.where(solver_side, hidden_ref[i], mine)
        if i > 0:
            whole_slope = slope[...].reshape(batch, width)

            @pl.loop(0, width // COLUMNS)
            def _(j):
                columns = columns_of(j)
                block = weights.at[i].reshape(width, width)[columns, :]
                back = lax.dot_general(
                    whole_slope,
                    block,
                    (((1,), (1,)), ((), ())),
                    preferred_element_type=jnp.float32,
                )
                residual[:, columns] = (back * factors[i - 1, :, columns]).astype(jnp.bfloat16)

        role_copies.append(
            send(
                payload_hidden.at[i],
                got_hidden_ref.at[i],
                role_send.at[role_slot],
                role_recv.at[role_slot],
                role_peer,
            )
        )
        role_slot += 1
        if i > 0:
            slope[...] = residual[...].reshape(slope.shape)
    hidden_keep = pltpu.make_async_copy(payload_hidden, sent_hidden_ref, local_sem.at[1])
    hidden_keep.start()
    for copy in role_copies:
        copy.wait_recv()
    for copy in sends:
        copy.wait_send()
    out_keep.wait()
    hidden_keep.wait()


def fused_training(features, hidden_narrow, out_narrow, own_fields, own_out, own_hidden, fields):
    layer_count, unit_rows, width = hidden_narrow.shape
    batch, cells = own_fields.shape
    groups = lax.axis_size("tile") // 4
    rows = batch // lax.axis_size("tile")
    narrow, wide = jnp.bfloat16, jnp.float32
    dma = pltpu.SemaphoreType.DMA
    vmem = pl.BlockSpec(memory_space=pltpu.VMEM)
    anywhere = pl.BlockSpec(memory_space=pl.ANY)
    parts = width // COLUMNS
    role_slots = 1 + cells // COLUMNS + layer_count
    return pl.pallas_call(
        functools.partial(train_kernel, groups),
        out_shape=(
            jax.ShapeDtypeStruct((width, cells), narrow),
            jax.ShapeDtypeStruct(hidden_narrow.shape, narrow),
            jax.ShapeDtypeStruct((width, cells), narrow),
            jax.ShapeDtypeStruct(hidden_narrow.shape, narrow),
            jax.ShapeDtypeStruct((batch, cells), narrow),
        ),
        in_specs=[anywhere, vmem] + [anywhere] * 3,
        out_specs=[anywhere] * 5,
        scratch_shapes=[
            pltpu.VMEM((batch, width), narrow),
            pltpu.VMEM((width, cells), narrow),
            pltpu.VMEM((batch, cells), wide),
            pltpu.VMEM((layer_count, groups, 2, 2, unit_rows, width), narrow),
            pltpu.VMEM((layer_count, batch, width), narrow),
            pltpu.VMEM((layer_count, batch, width), wide),
            pltpu.VMEM((batch, cells), narrow),
            pltpu.VMEM((groups, 2, 2, rows, width), wide),
            pltpu.VMEM((groups, 2, 2, rows, width), narrow),
            pltpu.VMEM((width, cells), narrow),
            pltpu.VMEM(hidden_narrow.shape, narrow),
            pltpu.VMEM((LANES, width), wide),
            pltpu.VMEM((groups, 2, rows, width), wide),
            pltpu.VMEM((groups, rows, width), narrow),
            pltpu.VMEM((groups, rows, width), narrow),
            pltpu.VMEM((groups, rows, width), narrow),
            pltpu.VMEM((groups - 1, rows, width), narrow),
            dma((layer_count, groups - 1)),
            dma((layer_count, groups - 1)),
            dma((layer_count, groups)),
            dma((layer_count, groups)),
            dma((layer_count,)),
            dma((layer_count,)),
            dma((parts, groups + 1)),
            dma((parts, groups + 1)),
            dma((parts, groups + 1)),
            dma((parts, groups + 1)),
            dma((role_slots,)),
            dma((role_slots,)),
            dma((4,)),
        ],
        compiler_params=pltpu.CompilerParams(
            collective_id=0, has_side_effects=True, vmem_limit_bytes=64000000
        ),
        cost_estimate=pl.CostEstimate(
            flops=60 * batch * width * width, bytes_accessed=40 * batch * width, transcendentals=0
        ),
    )(features, hidden_narrow, out_narrow, own_fields, fields)


def training(features, hidden_narrow, out_narrow, own_fields, own_out, own_hidden, fields):
    tiles = lax.axis_size("tile")
    fits = (
        tiles % 4 == 0
        and tiles > 4
        and (own_fields.shape[0] // tiles) % 16 == 0
        and LANES % own_hidden.shape[1] == 0
    )
    chosen = fused_training if fits else plain_training
    return chosen(features, hidden_narrow, out_narrow, own_fields, own_out, own_hidden, fields)


def body(fields_pair, velocity, growth, features, assignment, out_pair, hidden_pair):
    solver_side = lax.axis_index("role") == 0
    own_fields = fields_pair[0]
    own_out = out_pair[0]
    own_hidden = hidden_pair[0]
    stacked = jnp.concatenate([own_fields, velocity[None, :]], axis=0)
    advanced = advance(extended(stacked, "tile", 1, 1), growth)
    grad_out, grad_hidden, other_out, other_hidden, fresh_fields = training(
        features,
        own_hidden.astype(jnp.bfloat16),
        own_out.astype(jnp.bfloat16),
        own_fields,
        own_out,
        own_hidden,
        advanced.astype(jnp.bfloat16),
    )
    grad_out, grad_hidden, other_out, other_hidden = (
        v.astype(jnp.float32) for v in (grad_out, grad_hidden, other_out, other_hidden)
    )
    out_next = jnp.where(
        solver_side,
        momentum_decay * own_out + other_out,
        own_out - step_size * (momentum_decay * other_out + grad_out),
    )
    hidden_next = jnp.where(
        solver_side,
        momentum_decay * own_hidden + other_hidden,
        own_hidden - step_size * (momentum_decay * other_hidden + grad_hidden),
    )
    next_batch = jnp.take(fresh_fields, assignment, axis=0).astype(jnp.float32)
    fields_next = jnp.where(solver_side, advanced, next_batch)
    return (fields_next[None], out_next[None], hidden_next[None])


def solution(mesh):
    return jax.shard_map(
        body,
        mesh=mesh,
        in_specs=(
            P("role", None, "tile"),
            P("tile"),
            P("tile"),
            P(),
            P(),
            P("role", None, "tile"),
            P("role", None, "tile", None),
        ),
        out_specs=(P("role", None, "tile"), P("role", None, "tile"), P("role", None, "tile", None)),
        check_vma=False,
    )
```

```python
import functools

import jax
import jax.numpy as jnp
from jax import lax
from jax.experimental import pallas as pl
from jax.experimental.pallas import tpu as pltpu
from jax.sharding import PartitionSpec as P

momentum_decay = 0.9
step_size = 0.1


def extended(value, axis, dim, width):
    count, length = (lax.axis_size(axis), value.shape[dim])
    up = [(i, (i + 1) % count) for i in range(count)]
    down = [(j, i) for i, j in up]
    last = lax.slice_in_dim(value, length - width, length, axis=dim)
    leading = lax.slice_in_dim(value, 0, width, axis=dim)
    before = lax.ppermute(last, axis, up)
    after = lax.ppermute(leading, axis, down)
    return jnp.concatenate([before, value, after], axis=dim)


def silu_slope(values):
    logistic = jax.nn.sigmoid(values)
    return logistic * (1.0 + values * (1.0 - logistic))


def advance(padded, growth):
    states = padded[:-1]
    velocity_row = padded[-1]
    outflow = (
        jnp.maximum(velocity_row[:-1], 0.0) * states[:, :-1]
        + jnp.minimum(velocity_row[:-1], 0.0) * states[:, 1:]
    )
    carried = states[:, 1:-1] - outflow[:, 1:] + outflow[:, :-1]
    return carried + growth * carried * (1.0 - carried)


def to_trainer(value):
    return lax.ppermute(value.astype(jnp.bfloat16), "role", [(0, 1)])


def to_solver(value):
    return lax.ppermute(value.astype(jnp.bfloat16), "role", [(1, 0)])


def plain_training(features, hidden_narrow, out_narrow, own_fields, own_out, own_hidden, fields):
    layer_count, unit_rows = own_hidden.shape[:2]
    batch = own_fields.shape[0]
    first_unit = lax.axis_index("tile") * unit_rows
    momentum_out = to_trainer(own_out)
    momentum_hidden = to_trainer(own_hidden)
    full_hidden = [
        lax.all_gather(hidden_narrow[i], "tile", axis=0, tiled=True) for i in range(layer_count)
    ]
    inputs, summed_list = [], []
    activation = features
    for i in range(layer_count):
        inputs.append(activation)
        summed = jnp.dot(activation, full_hidden[i], preferred_element_type=jnp.float32)
        summed_list.append(summed)
        activation = jax.nn.silu(summed).astype(jnp.bfloat16)
    predicted = jnp.dot(activation, out_narrow, preferred_element_type=jnp.float32)
    residual = ((predicted - own_fields) / batch).astype(jnp.bfloat16)
    partial_grad = lax.dot_general(
        residual, out_narrow, (((1,), (1,)), ((), ())), preferred_element_type=jnp.float32
    )
    upstream = lax.psum(partial_grad, "tile")
    grad_out = jnp.dot(activation.T, residual, preferred_element_type=jnp.float32)
    sent_out = to_solver(grad_out)
    gradients, sent = [], []
    for i in reversed(range(layer_count)):
        slope = (upstream * silu_slope(summed_list[i])).astype(jnp.bfloat16)
        own_inputs = lax.dynamic_slice_in_dim(inputs[i], first_unit, unit_rows, 1)
        gradient = jnp.dot(own_inputs.T, slope, preferred_element_type=jnp.float32)
        gradients.append(gradient)
        sent.append(to_solver(gradient))
        if i > 0:
            upstream = lax.dot_general(
                slope, full_hidden[i], (((1,), (1,)), ((), ())), preferred_element_type=jnp.float32
            )
    solver_side = lax.axis_index("role") == 0
    grad_out = jnp.where(solver_side, sent_out.astype(jnp.float32), grad_out)
    other_hidden = jnp.where(solver_side, jnp.stack(sent[::-1]), momentum_hidden)
    return grad_out, jnp.stack(gradients[::-1]), momentum_out, other_hidden, to_trainer(fields)


LANES = 128
COLUMNS = 256


def train_kernel(
    groups,
    features_hbm,
    hidden_ref,
    out_hbm,
    target_hbm,
    fields_hbm,
    grad_out_ref,
    sent_hidden_ref,
    got_out_ref,
    got_hidden_ref,
    got_fields_ref,
    features_ref,
    out_ref,
    target_ref,
    weights,
    inputs,
    factors,
    residual,
    next_slope,
    got_residual,
    got_inputs,
    partial,
    slope,
    payload,
    payload_hidden,
    gradient,
    core_sum,
    x_away,
    x_sum,
    z_away,
    z_sum,
    z_send,
    z_recv,
    x_send,
    x_recv,
    core_send,
    core_recv,
    sum_send,
    sum_recv,
    slope_send,
    slope_recv,
    role_send,
    role_recv,
    local_sem,
):
    layer_count, unit_rows, width = hidden_ref.shape
    batch, cells = target_ref.shape
    rows = partial.shape[3]
    role = lax.axis_index("role")
    tile = lax.axis_index("tile")
    core = lax.rem(tile, 2)
    x = lax.rem(tile // 2, 2)
    z = tile // 4
    solver_side = role == 0

    def device(z_at, x_at, core_at):
        return (role, z_at * 4 + x_at * 2 + core_at)

    z_places = [lax.rem(z + k, groups) for k in range(1, groups)]
    z_origins = [lax.rem(z + groups - k, groups) for k in range(1, groups)]
    z_peers = [device(place, x, core) for place in z_places]
    x_peer = device(z, 1 - x, core)
    core_peer = device(z, x, 1 - core)
    role_peer = (1 - role, tile)
    sends = []

    def send(source, target, send_sem, recv_sem, peer):
        copy = pltpu.make_async_remote_copy(
            src_ref=source,
            dst_ref=target,
            send_sem=send_sem,
            recv_sem=recv_sem,
            device_id=peer,
            device_id_type=pl.DeviceIdType.MESH,
        )
        copy.start()
        sends.append(copy)
        return copy

    own = pltpu.make_async_copy(hidden_ref, weights.at[:, z, x, core], local_sem.at[0])
    own.start()
    loads = [
        pltpu.make_async_copy(features_hbm, features_ref, local_sem.at[1]),
        pltpu.make_async_copy(out_hbm, out_ref, local_sem.at[2]),
        pltpu.make_async_copy(target_hbm, target_ref, local_sem.at[3]),
    ]
    for load in loads:
        load.start()
    barrier = pltpu.get_barrier_semaphore()
    peers = z_peers + [x_peer, core_peer, role_peer]
    for peer in peers:
        pl.semaphore_signal(barrier, inc=1, device_id=peer, device_id_type=pl.DeviceIdType.MESH)
    pl.semaphore_wait(barrier, len(peers))

    x_copies = [[] for _ in range(layer_count)]

    def send_x(i, slot, source, place):
        x_copies[i].append(
            send(
                source,
                weights.at[i, place, x, core],
                x_send.at[i, slot],
                x_recv.at[i, slot],
                x_peer,
            )
        )

    z_copies = []
    for i in range(layer_count):
        z_copies.append(
            [
                send(
                    hidden_ref.at[i],
                    weights.at[i, z, x, core],
                    z_send.at[i, k],
                    z_recv.at[i, k],
                    z_peers[k],
                )
                for k in range(groups - 1)
            ]
        )
        if i < 2:
            send_x(i, 0, hidden_ref.at[i], z)
    last = layer_count - 1
    role_copies = []

    def send_role(source, target):
        slot = len(role_copies)
        copy = send(source, target, role_send.at[slot], role_recv.at[slot], role_peer)
        role_copies.append(copy)
        return copy

    send_role(fields_hbm, got_fields_ref)
    send_role(out_hbm, got_out_ref)
    own.wait()
    for load in loads:
        load.wait()

    def columns_of(j):
        return pl.ds(pl.multiple_of(j * COLUMNS, COLUMNS), COLUMNS)

    def forward(i):
        @pl.loop(0, width // COLUMNS)
        def _(j):
            columns = columns_of(j)
            block = weights[i, :, :, :, :, columns].reshape(width, COLUMNS)
            activation = features_ref[...] if i == 0 else inputs[i - 1]
            summed = jnp.dot(activation, block, preferred_element_type=jnp.float32)
            logistic = jax.nn.sigmoid(summed)
            inputs[i, :, columns] = (summed * logistic).astype(jnp.bfloat16)
            factors[i, :, columns] = logistic * (1.0 + summed * (1.0 - logistic))

    core_copies = [[] for _ in range(layer_count)]

    def send_core(i, place, x_at, source=None):
        slot = len(core_copies[i])
        view = weights.at[i, place, x_at, core]
        core_copies[i].append(
            send(
                view if source is None else source,
                view,
                core_send.at[i, slot],
                core_recv.at[i, slot],
                core_peer,
            )
        )

    for i in range(layer_count):
        send_core(i, z, x, hidden_ref.at[i])
    for i in range(layer_count + 2):
        if i < layer_count:
            for k in range(groups - 1):
                z_copies[i][k].wait_recv()
                send_x(i, k + 1, weights.at[i, z_origins[k], x, core], z_origins[k])
                send_core(i, z_origins[k], x)
            if i + 2 < layer_count:
                send_x(i + 2, 0, hidden_ref.at[i + 2], z)
        if 1 <= i <= layer_count:
            for slot, place in enumerate([z] + z_origins):
                x_copies[i - 1][slot].wait_recv()
                send_core(i - 1, place, 1 - x)
        if i >= 2:
            for copy in core_copies[i - 2]:
                copy.wait_recv()
            forward(i - 2)

    half = batch // 2
    half_rows = pl.ds(pl.multiple_of(core * half, half), half)
    inputs_copy = send_role(inputs.at[last, half_rows, :], got_inputs.at[half_rows, :])
    chunks = [pl.ds(j * COLUMNS, COLUMNS) for j in range(cells // COLUMNS)]
    for columns in chunks:
        predicted = jnp.dot(inputs[last], out_ref[:, columns], preferred_element_type=jnp.float32)
        residual[:, columns] = ((predicted - target_ref[:, columns]) / batch).astype(jnp.bfloat16)
        send_role(residual.at[:, columns], got_residual.at[:, columns])

    parts = [pl.ds(j * COLUMNS, COLUMNS) for j in range(width // COLUMNS)]
    core_sums, x_sums, z_sums, z_slopes, x_slopes, core_slopes = [], [], [], [], [], []
    for j, columns in enumerate(parts):
        part = lax.dot_general(
            residual[...],
            out_ref[columns, :],
            (((1,), (1,)), ((), ())),
            preferred_element_type=jnp.float32,
        )
        partial[:, :, :, :, columns] = part.reshape(groups, 2, 2, rows, COLUMNS)
        core_sums.append(
            send(
                partial.at[:, :, 1 - core, :, columns],
                core_sum.at[:, :, :, columns],
                sum_send.at[j, 0],
                sum_recv.at[j, 0],
                core_peer,
            )
        )
    for j, columns in enumerate(parts):
        core_sums[j].wait_recv()
        away = partial[:, 1 - x, core, :, columns] + core_sum[:, 1 - x, :, columns]
        x_away[:, :, columns] = away.astype(jnp.bfloat16)
        x_sums.append(
            send(
                x_away.at[:, :, columns],
                x_sum.at[:, :, columns],
                sum_send.at[j, 1],
                sum_recv.at[j, 1],
                x_peer,
            )
        )
    for j, columns in enumerate(parts):
        kept = partial[:, x, core, :, columns] + core_sum[:, x, :, columns]
        x_sums[j].wait_recv()
        kept = kept + x_sum[:, :, columns].astype(jnp.float32)
        partial[:, x, core, :, columns] = kept
        z_away[:, :, columns] = kept.astype(jnp.bfloat16)
        z_sums.append(
            [
                send(
                    z_away.at[z_places[k], :, columns],
                    z_sum.at[k, :, columns],
                    sum_send.at[j, 2 + k],
                    sum_recv.at[j, 2 + k],
                    z_peers[k],
                )
                for k in range(groups - 1)
            ]
        )
    own_rows = pl.ds(pl.multiple_of(tile * rows, rows), rows)

    def send_slope(view, j, slot, peer):
        return send(view, view, slope_send.at[j, slot], slope_recv.at[j, slot], peer)

    for j, columns in enumerate(parts):
        upstream = partial[z, x, core, :, columns]
        for k in range(groups - 1):
            z_sums[j][k].wait_recv()
            upstream = upstream + z_sum[k, :, columns].astype(jnp.float32)
        slope[z, x, core, :, columns] = (upstream * factors[last, own_rows, columns]).astype(
            jnp.bfloat16
        )
        view = slope.at[z, x, core, :, columns]
        z_slopes.append([send_slope(view, j, k, z_peers[k]) for k in range(groups - 1)])
    for j, columns in enumerate(parts):
        for copy in z_slopes[j]:
            copy.wait_recv()
        view = slope.at[:, x, core, :, columns]
        x_slopes.append(send_slope(view, j, groups - 1, x_peer))
    for j, columns in enumerate(parts):
        x_slopes[j].wait_recv()
        core_slopes.append(send_slope(slope.at[:, :, core, :, columns], j, groups, core_peer))
    for copy in core_slopes:
        copy.wait_recv()
    for copies in z_slopes + [x_slopes, core_slopes]:
        for copy in copies:
            copy.wait_send()
            sends[:] = [other for other in sends if other is not copy]

    inputs_copy.wait_recv()
    view = got_inputs.at[half_rows, :]
    inputs_swap = send(view, view, local_sem.at[0], local_sem.at[2], core_peer)

    per_block = LANES // unit_rows
    first_lane = pl.multiple_of((tile // per_block) * LANES, LANES)
    unit_first = pl.multiple_of(lax.rem(tile, per_block) * unit_rows, unit_rows)
    for i in reversed(range(layer_count)):
        source = features_ref if i == 0 else inputs.at[i - 1]
        own_inputs = source[:, pl.ds(first_lane, LANES)]

        @pl.loop(0, width // COLUMNS)
        def _(j):
            columns = columns_of(j)
            gradient[:, columns] = lax.dot_general(
                own_inputs,
                slope[:, :, :, :, columns].reshape(batch, COLUMNS),
                (((0,), (0,)), ((), ())),
                preferred_element_type=jnp.float32,
            )

        mine = gradient[pl.ds(unit_first, unit_rows), :].astype(jnp.bfloat16)
        payload_hidden[i] = jnp.where(solver_side, hidden_ref[i], mine)
        if i > 0:
            whole_slope = slope[...].reshape(batch, width)

            @pl.loop(0, width // COLUMNS)
            def _(j):
                columns = columns_of(j)
                block = weights.at[i].reshape(width, width)[columns, :]
                back = lax.dot_general(
                    whole_slope,
                    block,
                    (((1,), (1,)), ((), ())),
                    preferred_element_type=jnp.float32,
                )
                next_slope[:, columns] = (back * factors[i - 1, :, columns]).astype(jnp.bfloat16)

        send_role(payload_hidden.at[i], got_hidden_ref.at[i])
        if i > 0:
            slope[...] = next_slope[...].reshape(slope.shape)
    hidden_keep = pltpu.make_async_copy(payload_hidden, sent_hidden_ref, local_sem.at[1])
    hidden_keep.start()
    inputs_swap.wait_recv()
    for copy in role_copies:
        if copy is not inputs_copy:
            copy.wait_recv()
    chosen = jnp.where(solver_side, got_inputs[...], inputs[last])
    keeps = [hidden_keep]
    for j, columns in enumerate(chunks):
        grad = lax.dot_general(
            chosen,
            jnp.where(solver_side, got_residual[:, columns], residual[:, columns]),
            (((0,), (0,)), ((), ())),
            preferred_element_type=jnp.float32,
        )
        payload[:, columns] = grad.astype(jnp.bfloat16)
        keep = pltpu.make_async_copy(
            payload.at[:, columns], grad_out_ref.at[:, columns], local_sem.at[4 + j]
        )
        keep.start()
        keeps.append(keep)
    for copy in sends:
        copy.wait_send()
    for keep in keeps:
        keep.wait()


def fused_training(features, hidden_narrow, out_narrow, own_fields, own_out, own_hidden, fields):
    layer_count, unit_rows, width = hidden_narrow.shape
    batch, cells = own_fields.shape
    groups = lax.axis_size("tile") // 4
    rows = batch // lax.axis_size("tile")
    narrow, wide = jnp.bfloat16, jnp.float32
    dma = pltpu.SemaphoreType.DMA
    vmem = pl.BlockSpec(memory_space=pltpu.VMEM)
    anywhere = pl.BlockSpec(memory_space=pl.ANY)
    parts = width // COLUMNS
    role_slots = 3 + cells // COLUMNS + layer_count
    return pl.pallas_call(
        functools.partial(train_kernel, groups),
        out_shape=(
            jax.ShapeDtypeStruct((width, cells), narrow),
            jax.ShapeDtypeStruct(hidden_narrow.shape, narrow),
            jax.ShapeDtypeStruct((width, cells), narrow),
            jax.ShapeDtypeStruct(hidden_narrow.shape, narrow),
            jax.ShapeDtypeStruct((batch, cells), narrow),
        ),
        in_specs=[anywhere, vmem] + [anywhere] * 3,
        out_specs=[anywhere] * 5,
        scratch_shapes=[
            pltpu.VMEM((batch, width), narrow),
            pltpu.VMEM((width, cells), narrow),
            pltpu.VMEM((batch, cells), wide),
            pltpu.VMEM((layer_count, groups, 2, 2, unit_rows, width), narrow),
            pltpu.VMEM((layer_count, batch, width), narrow),
            pltpu.VMEM((layer_count, batch, width), wide),
            pltpu.VMEM((batch, cells), narrow),
            pltpu.VMEM((batch, width), narrow),
            pltpu.VMEM((batch, cells), narrow),
            pltpu.VMEM((batch, width), narrow),
            pltpu.VMEM((groups, 2, 2, rows, width), wide),
            pltpu.VMEM((groups, 2, 2, rows, width), narrow),
            pltpu.VMEM((width, cells), narrow),
            pltpu.VMEM(hidden_narrow.shape, narrow),
            pltpu.VMEM((LANES, width), wide),
            pltpu.VMEM((groups, 2, rows, width), wide),
            pltpu.VMEM((groups, rows, width), narrow),
            pltpu.VMEM((groups, rows, width), narrow),
            pltpu.VMEM((groups, rows, width), narrow),
            pltpu.VMEM((groups - 1, rows, width), narrow),
            dma((layer_count, groups - 1)),
            dma((layer_count, groups - 1)),
            dma((layer_count, groups)),
            dma((layer_count, groups)),
            dma((layer_count, 2 * groups)),
            dma((layer_count, 2 * groups)),
            dma((parts, groups + 1)),
            dma((parts, groups + 1)),
            dma((parts, groups + 1)),
            dma((parts, groups + 1)),
            dma((role_slots,)),
            dma((role_slots,)),
            dma((4 + cells // COLUMNS,)),
        ],
        compiler_params=pltpu.CompilerParams(
            collective_id=0, has_side_effects=True, vmem_limit_bytes=64000000
        ),
        cost_estimate=pl.CostEstimate(
            flops=60 * batch * width * width, bytes_accessed=40 * batch * width, transcendentals=0
        ),
    )(features, hidden_narrow, out_narrow, own_fields, fields)


def training(features, hidden_narrow, out_narrow, own_fields, own_out, own_hidden, fields):
    tiles = lax.axis_size("tile")
    fits = (
        tiles % 4 == 0
        and tiles > 4
        and (own_fields.shape[0] // tiles) % 16 == 0
        and LANES % own_hidden.shape[1] == 0
    )
    chosen = fused_training if fits else plain_training
    return chosen(features, hidden_narrow, out_narrow, own_fields, own_out, own_hidden, fields)


def body(fields_pair, velocity, growth, features, assignment, out_pair, hidden_pair):
    solver_side = lax.axis_index("role") == 0
    own_fields = fields_pair[0]
    own_out = out_pair[0]
    own_hidden = hidden_pair[0]
    stacked = jnp.concatenate([own_fields, velocity[None, :]], axis=0)
    advanced = advance(extended(stacked, "tile", 1, 1), growth)
    grad_out, grad_hidden, other_out, other_hidden, fresh_fields = training(
        features,
        own_hidden.astype(jnp.bfloat16),
        own_out.astype(jnp.bfloat16),
        own_fields,
        own_out,
        own_hidden,
        advanced.astype(jnp.bfloat16),
    )
    grad_out, grad_hidden, other_out, other_hidden = (
        v.astype(jnp.float32) for v in (grad_out, grad_hidden, other_out, other_hidden)
    )
    out_next = jnp.where(
        solver_side,
        momentum_decay * own_out + grad_out,
        own_out - step_size * (momentum_decay * other_out + grad_out),
    )
    hidden_next = jnp.where(
        solver_side,
        momentum_decay * own_hidden + other_hidden,
        own_hidden - step_size * (momentum_decay * other_hidden + grad_hidden),
    )
    next_batch = jnp.take(fresh_fields, assignment, axis=0).astype(jnp.float32)
    fields_next = jnp.where(solver_side, advanced, next_batch)
    return (fields_next[None], out_next[None], hidden_next[None])


def solution(mesh):
    return jax.shard_map(
        body,
        mesh=mesh,
        in_specs=(
            P("role", None, "tile"),
            P("tile"),
            P("tile"),
            P(),
            P(),
            P("role", None, "tile"),
            P("role", None, "tile", None),
        ),
        out_specs=(P("role", None, "tile"), P("role", None, "tile"), P("role", None, "tile", None)),
        check_vma=False,
    )
```

```python
import functools

import jax
import jax.numpy as jnp
from jax import lax
from jax.experimental import pallas as pl
from jax.experimental.pallas import tpu as pltpu
from jax.sharding import PartitionSpec as P

momentum_decay = 0.9
step_size = 0.1


def extended(value, axis, dim, width):
    count, length = (lax.axis_size(axis), value.shape[dim])
    up = [(i, (i + 1) % count) for i in range(count)]
    down = [(j, i) for i, j in up]
    last = lax.slice_in_dim(value, length - width, length, axis=dim)
    leading = lax.slice_in_dim(value, 0, width, axis=dim)
    before = lax.ppermute(last, axis, up)
    after = lax.ppermute(leading, axis, down)
    return jnp.concatenate([before, value, after], axis=dim)


def silu_slope(values):
    logistic = jax.nn.sigmoid(values)
    return logistic * (1.0 + values * (1.0 - logistic))


def advance(padded, growth):
    states = padded[:-1]
    velocity_row = padded[-1]
    outflow = (
        jnp.maximum(velocity_row[:-1], 0.0) * states[:, :-1]
        + jnp.minimum(velocity_row[:-1], 0.0) * states[:, 1:]
    )
    carried = states[:, 1:-1] - outflow[:, 1:] + outflow[:, :-1]
    return carried + growth * carried * (1.0 - carried)


def to_trainer(value):
    return lax.ppermute(value.astype(jnp.bfloat16), "role", [(0, 1)])


def to_solver(value):
    return lax.ppermute(value.astype(jnp.bfloat16), "role", [(1, 0)])


def plain_training(features, hidden_narrow, out_narrow, own_fields, own_out, own_hidden, fields):
    layer_count, unit_rows = own_hidden.shape[:2]
    batch = own_fields.shape[0]
    first_unit = lax.axis_index("tile") * unit_rows
    momentum_out = to_trainer(own_out)
    momentum_hidden = to_trainer(own_hidden)
    full_hidden = [
        lax.all_gather(hidden_narrow[i], "tile", axis=0, tiled=True) for i in range(layer_count)
    ]
    inputs, summed_list = [], []
    activation = features
    for i in range(layer_count):
        inputs.append(activation)
        summed = jnp.dot(activation, full_hidden[i], preferred_element_type=jnp.float32)
        summed_list.append(summed)
        activation = jax.nn.silu(summed).astype(jnp.bfloat16)
    predicted = jnp.dot(activation, out_narrow, preferred_element_type=jnp.float32)
    residual = ((predicted - own_fields) / batch).astype(jnp.bfloat16)
    partial_grad = lax.dot_general(
        residual, out_narrow, (((1,), (1,)), ((), ())), preferred_element_type=jnp.float32
    )
    upstream = lax.psum(partial_grad, "tile")
    grad_out = jnp.dot(activation.T, residual, preferred_element_type=jnp.float32)
    sent_out = to_solver(grad_out)
    gradients, sent = [], []
    for i in reversed(range(layer_count)):
        slope = (upstream * silu_slope(summed_list[i])).astype(jnp.bfloat16)
        own_inputs = lax.dynamic_slice_in_dim(inputs[i], first_unit, unit_rows, 1)
        gradient = jnp.dot(own_inputs.T, slope, preferred_element_type=jnp.float32)
        gradients.append(gradient)
        sent.append(to_solver(gradient))
        if i > 0:
            upstream = lax.dot_general(
                slope, full_hidden[i], (((1,), (1,)), ((), ())), preferred_element_type=jnp.float32
            )
    solver_side = lax.axis_index("role") == 0
    grad_out = jnp.where(solver_side, sent_out.astype(jnp.float32), grad_out)
    other_hidden = jnp.where(solver_side, jnp.stack(sent[::-1]), momentum_hidden)
    return grad_out, jnp.stack(gradients[::-1]), momentum_out, other_hidden, to_trainer(fields)


LANES = 128
COLUMNS = 256


def train_kernel(
    groups,
    features_hbm,
    hidden_ref,
    out_hbm,
    target_hbm,
    fields_hbm,
    grad_out_ref,
    sent_hidden_ref,
    got_out_ref,
    got_hidden_ref,
    got_fields_ref,
    features_ref,
    out_ref,
    target_ref,
    weights,
    inputs,
    factors,
    residual,
    next_slope,
    got_residual,
    got_inputs,
    partial,
    slope,
    payload,
    payload_hidden,
    gradient,
    core_sum,
    x_away,
    x_sum,
    z_away,
    z_sum,
    z_send,
    z_recv,
    x_send,
    x_recv,
    core_send,
    core_recv,
    sum_send,
    sum_recv,
    slope_send,
    slope_recv,
    role_send,
    role_recv,
    local_sem,
):
    layer_count, unit_rows, width = hidden_ref.shape
    batch, cells = target_ref.shape
    rows = partial.shape[3]
    role = lax.axis_index("role")
    tile = lax.axis_index("tile")
    core = lax.rem(tile, 2)
    x = lax.rem(tile // 2, 2)
    z = tile // 4
    solver_side = role == 0

    def device(z_at, x_at, core_at):
        return (role, z_at * 4 + x_at * 2 + core_at)

    z_places = [lax.rem(z + k, groups) for k in range(1, groups)]
    z_origins = [lax.rem(z + groups - k, groups) for k in range(1, groups)]
    z_peers = [device(place, x, core) for place in z_places]
    x_peer = device(z, 1 - x, core)
    core_peer = device(z, x, 1 - core)
    role_peer = (1 - role, tile)
    sends = []

    def send(source, target, send_sem, recv_sem, peer):
        copy = pltpu.make_async_remote_copy(
            src_ref=source,
            dst_ref=target,
            send_sem=send_sem,
            recv_sem=recv_sem,
            device_id=peer,
            device_id_type=pl.DeviceIdType.MESH,
        )
        copy.start()
        sends.append(copy)
        return copy

    own = pltpu.make_async_copy(hidden_ref, weights.at[:, z, x, core], local_sem.at[0])
    own.start()
    loads = [
        pltpu.make_async_copy(features_hbm, features_ref, local_sem.at[1]),
        pltpu.make_async_copy(out_hbm, out_ref, local_sem.at[2]),
        pltpu.make_async_copy(target_hbm, target_ref, local_sem.at[3]),
    ]
    for load in loads:
        load.start()
    barrier = pltpu.get_barrier_semaphore()
    peers = z_peers + [x_peer, core_peer, role_peer]
    for peer in peers:
        pl.semaphore_signal(barrier, inc=1, device_id=peer, device_id_type=pl.DeviceIdType.MESH)
    pl.semaphore_wait(barrier, len(peers))

    x_copies = [[] for _ in range(layer_count)]

    def send_x(i, slot, source, place):
        x_copies[i].append(
            send(
                source,
                weights.at[i, place, x, core],
                x_send.at[i, slot],
                x_recv.at[i, slot],
                x_peer,
            )
        )

    z_copies = []
    for i in range(layer_count):
        z_copies.append(
            [
                send(
                    hidden_ref.at[i],
                    weights.at[i, z, x, core],
                    z_send.at[i, k],
                    z_recv.at[i, k],
                    z_peers[k],
                )
                for k in range(groups - 1)
            ]
        )
        if i < 3:
            send_x(i, 0, hidden_ref.at[i], z)
    last = layer_count - 1
    role_copies = []

    def send_role(source, target):
        slot = len(role_copies)
        copy = send(source, target, role_send.at[slot], role_recv.at[slot], role_peer)
        role_copies.append(copy)
        return copy

    send_role(fields_hbm, got_fields_ref)
    send_role(out_hbm, got_out_ref)
    own.wait()
    for load in loads:
        load.wait()

    def columns_of(j):
        return pl.ds(pl.multiple_of(j * COLUMNS, COLUMNS), COLUMNS)

    def forward(i):
        @pl.loop(0, width // COLUMNS)
        def _(j):
            columns = columns_of(j)
            block = weights[i, :, :, :, :, columns].reshape(width, COLUMNS)
            activation = features_ref[...] if i == 0 else inputs[i - 1]
            summed = jnp.dot(activation, block, preferred_element_type=jnp.float32)
            logistic = jax.nn.sigmoid(summed)
            inputs[i, :, columns] = (summed * logistic).astype(jnp.bfloat16)
            factors[i, :, columns] = logistic * (1.0 + summed * (1.0 - logistic))

    core_copies = [[] for _ in range(layer_count)]

    def send_core(i, place, x_at, source=None):
        slot = len(core_copies[i])
        view = weights.at[i, place, x_at, core]
        core_copies[i].append(
            send(
                view if source is None else source,
                view,
                core_send.at[i, slot],
                core_recv.at[i, slot],
                core_peer,
            )
        )

    for i in range(layer_count):
        send_core(i, z, x, hidden_ref.at[i])
    for i in range(layer_count + 2):
        if i < layer_count:
            for k in range(groups - 1):
                z_copies[i][k].wait_recv()
                send_x(i, k + 1, weights.at[i, z_origins[k], x, core], z_origins[k])
                send_core(i, z_origins[k], x)
            if i + 3 < layer_count:
                send_x(i + 3, 0, hidden_ref.at[i + 3], z)
        if 1 <= i <= layer_count:
            for slot, place in enumerate([z] + z_origins):
                x_copies[i - 1][slot].wait_recv()
                send_core(i - 1, place, 1 - x)
        if i >= 2:
            for copy in core_copies[i - 2]:
                copy.wait_recv()
            forward(i - 2)

    half = batch // 2
    half_rows = pl.ds(pl.multiple_of(core * half, half), half)
    inputs_copy = send_role(inputs.at[last, half_rows, :], got_inputs.at[half_rows, :])
    chunks = [pl.ds(j * COLUMNS, COLUMNS) for j in range(cells // COLUMNS)]
    residual_copies = []
    for columns in chunks:
        predicted = jnp.dot(inputs[last], out_ref[:, columns], preferred_element_type=jnp.float32)
        residual[:, columns] = ((predicted - target_ref[:, columns]) / batch).astype(jnp.bfloat16)
        residual_copies.append(send_role(residual.at[:, columns], got_residual.at[:, columns]))

    parts = [pl.ds(j * COLUMNS, COLUMNS) for j in range(width // COLUMNS)]
    core_sums, x_sums, z_sums, z_slopes, x_slopes, core_slopes = [], [], [], [], [], []
    for j, columns in enumerate(parts):
        part = lax.dot_general(
            residual[...],
            out_ref[columns, :],
            (((1,), (1,)), ((), ())),
            preferred_element_type=jnp.float32,
        )
        partial[:, :, :, :, columns] = part.reshape(groups, 2, 2, rows, COLUMNS)
        core_sums.append(
            send(
                partial.at[:, :, 1 - core, :, columns],
                core_sum.at[:, :, :, columns],
                sum_send.at[j, 0],
                sum_recv.at[j, 0],
                core_peer,
            )
        )
    for j, columns in enumerate(parts):
        core_sums[j].wait_recv()
        away = partial[:, 1 - x, core, :, columns] + core_sum[:, 1 - x, :, columns]
        x_away[:, :, columns] = away.astype(jnp.bfloat16)
        x_sums.append(
            send(
                x_away.at[:, :, columns],
                x_sum.at[:, :, columns],
                sum_send.at[j, 1],
                sum_recv.at[j, 1],
                x_peer,
            )
        )
    for j, columns in enumerate(parts):
        kept = partial[:, x, core, :, columns] + core_sum[:, x, :, columns]
        x_sums[j].wait_recv()
        kept = kept + x_sum[:, :, columns].astype(jnp.float32)
        partial[:, x, core, :, columns] = kept
        z_away[:, :, columns] = kept.astype(jnp.bfloat16)
        z_sums.append(
            [
                send(
                    z_away.at[z_places[k], :, columns],
                    z_sum.at[k, :, columns],
                    sum_send.at[j, 2 + k],
                    sum_recv.at[j, 2 + k],
                    z_peers[k],
                )
                for k in range(groups - 1)
            ]
        )
    own_rows = pl.ds(pl.multiple_of(tile * rows, rows), rows)

    def send_slope(view, j, slot, peer):
        return send(view, view, slope_send.at[j, slot], slope_recv.at[j, slot], peer)

    for j, columns in enumerate(parts):
        upstream = partial[z, x, core, :, columns]
        for k in range(groups - 1):
            z_sums[j][k].wait_recv()
            upstream = upstream + z_sum[k, :, columns].astype(jnp.float32)
        slope[z, x, core, :, columns] = (upstream * factors[last, own_rows, columns]).astype(
            jnp.bfloat16
        )
        view = slope.at[z, x, core, :, columns]
        z_slopes.append([send_slope(view, j, k, z_peers[k]) for k in range(groups - 1)])
    for j, columns in enumerate(parts):
        for copy in z_slopes[j]:
            copy.wait_recv()
        view = slope.at[:, x, core, :, columns]
        x_slopes.append(send_slope(view, j, groups - 1, x_peer))
    for j, columns in enumerate(parts):
        x_slopes[j].wait_recv()
        core_slopes.append(send_slope(slope.at[:, :, core, :, columns], j, groups, core_peer))
    for copy in core_slopes:
        copy.wait_recv()
    for copies in z_slopes + [x_slopes, core_slopes]:
        for copy in copies:
            copy.wait_send()
            sends[:] = [other for other in sends if other is not copy]

    inputs_copy.wait_recv()
    view = got_inputs.at[half_rows, :]
    inputs_swap = send(view, view, local_sem.at[0], local_sem.at[2], core_peer)

    per_block = LANES // unit_rows
    first_lane = pl.multiple_of((tile // per_block) * LANES, LANES)
    unit_first = pl.multiple_of(lax.rem(tile, per_block) * unit_rows, unit_rows)
    for i in reversed(range(layer_count)):
        source = features_ref if i == 0 else inputs.at[i - 1]
        own_inputs = source[:, pl.ds(first_lane, LANES)]

        @pl.loop(0, width // COLUMNS)
        def _(j):
            columns = columns_of(j)
            gradient[:, columns] = lax.dot_general(
                own_inputs,
                slope[:, :, :, :, columns].reshape(batch, COLUMNS),
                (((0,), (0,)), ((), ())),
                preferred_element_type=jnp.float32,
            )

        mine = gradient[pl.ds(unit_first, unit_rows), :].astype(jnp.bfloat16)
        payload_hidden[i] = jnp.where(solver_side, hidden_ref[i], mine)
        if i > 0:
            whole_slope = slope[...].reshape(batch, width)

            @pl.loop(0, width // COLUMNS)
            def _(j):
                columns = columns_of(j)
                block = weights.at[i].reshape(width, width)[columns, :]
                back = lax.dot_general(
                    whole_slope,
                    block,
                    (((1,), (1,)), ((), ())),
                    preferred_element_type=jnp.float32,
                )
                next_slope[:, columns] = (back * factors[i - 1, :, columns]).astype(jnp.bfloat16)

        send_role(payload_hidden.at[i], got_hidden_ref.at[i])
        if i > 0:
            slope[...] = next_slope[...].reshape(slope.shape)
    hidden_keep = pltpu.make_async_copy(payload_hidden, sent_hidden_ref, local_sem.at[1])
    hidden_keep.start()
    inputs_swap.wait_recv()
    for copy in residual_copies:
        copy.wait_recv()
    chosen = jnp.where(solver_side, got_inputs[...], inputs[last])
    keeps = [hidden_keep]
    for j, columns in enumerate(chunks):
        grad = lax.dot_general(
            chosen,
            jnp.where(solver_side, got_residual[:, columns], residual[:, columns]),
            (((0,), (0,)), ((), ())),
            preferred_element_type=jnp.float32,
        )
        payload[:, columns] = grad.astype(jnp.bfloat16)
        keep = pltpu.make_async_copy(
            payload.at[:, columns], grad_out_ref.at[:, columns], local_sem.at[4 + j]
        )
        keep.start()
        keeps.append(keep)
    waited = [inputs_copy] + residual_copies
    for copy in role_copies:
        if not any(copy is other for other in waited):
            copy.wait_recv()
    for copy in sends:
        copy.wait_send()
    for keep in keeps:
        keep.wait()


def fused_training(features, hidden_narrow, out_narrow, own_fields, own_out, own_hidden, fields):
    layer_count, unit_rows, width = hidden_narrow.shape
    batch, cells = own_fields.shape
    groups = lax.axis_size("tile") // 4
    rows = batch // lax.axis_size("tile")
    narrow, wide = jnp.bfloat16, jnp.float32
    dma = pltpu.SemaphoreType.DMA
    vmem = pl.BlockSpec(memory_space=pltpu.VMEM)
    anywhere = pl.BlockSpec(memory_space=pl.ANY)
    parts = width // COLUMNS
    role_slots = 3 + cells // COLUMNS + layer_count
    return pl.pallas_call(
        functools.partial(train_kernel, groups),
        out_shape=(
            jax.ShapeDtypeStruct((width, cells), narrow),
            jax.ShapeDtypeStruct(hidden_narrow.shape, narrow),
            jax.ShapeDtypeStruct((width, cells), narrow),
            jax.ShapeDtypeStruct(hidden_narrow.shape, narrow),
            jax.ShapeDtypeStruct((batch, cells), narrow),
        ),
        in_specs=[anywhere, vmem] + [anywhere] * 3,
        out_specs=[anywhere] * 5,
        scratch_shapes=[
            pltpu.VMEM((batch, width), narrow),
            pltpu.VMEM((width, cells), narrow),
            pltpu.VMEM((batch, cells), wide),
            pltpu.VMEM((layer_count, groups, 2, 2, unit_rows, width), narrow),
            pltpu.VMEM((layer_count, batch, width), narrow),
            pltpu.VMEM((layer_count, batch, width), wide),
            pltpu.VMEM((batch, cells), narrow),
            pltpu.VMEM((batch, width), narrow),
            pltpu.VMEM((batch, cells), narrow),
            pltpu.VMEM((batch, width), narrow),
            pltpu.VMEM((groups, 2, 2, rows, width), wide),
            pltpu.VMEM((groups, 2, 2, rows, width), narrow),
            pltpu.VMEM((width, cells), narrow),
            pltpu.VMEM(hidden_narrow.shape, narrow),
            pltpu.VMEM((LANES, width), wide),
            pltpu.VMEM((groups, 2, rows, width), wide),
            pltpu.VMEM((groups, rows, width), narrow),
            pltpu.VMEM((groups, rows, width), narrow),
            pltpu.VMEM((groups, rows, width), narrow),
            pltpu.VMEM((groups - 1, rows, width), narrow),
            dma((layer_count, groups - 1)),
            dma((layer_count, groups - 1)),
            dma((layer_count, groups)),
            dma((layer_count, groups)),
            dma((layer_count, 2 * groups)),
            dma((layer_count, 2 * groups)),
            dma((parts, groups + 1)),
            dma((parts, groups + 1)),
            dma((parts, groups + 1)),
            dma((parts, groups + 1)),
            dma((role_slots,)),
            dma((role_slots,)),
            dma((4 + cells // COLUMNS,)),
        ],
        compiler_params=pltpu.CompilerParams(
            collective_id=0, has_side_effects=True, vmem_limit_bytes=64000000
        ),
        cost_estimate=pl.CostEstimate(
            flops=60 * batch * width * width, bytes_accessed=40 * batch * width, transcendentals=0
        ),
    )(features, hidden_narrow, out_narrow, own_fields, fields)


def training(features, hidden_narrow, out_narrow, own_fields, own_out, own_hidden, fields):
    tiles = lax.axis_size("tile")
    fits = (
        tiles % 4 == 0
        and tiles > 4
        and (own_fields.shape[0] // tiles) % 16 == 0
        and LANES % own_hidden.shape[1] == 0
    )
    chosen = fused_training if fits else plain_training
    return chosen(features, hidden_narrow, out_narrow, own_fields, own_out, own_hidden, fields)


def body(fields_pair, velocity, growth, features, assignment, out_pair, hidden_pair):
    solver_side = lax.axis_index("role") == 0
    own_fields = fields_pair[0]
    own_out = out_pair[0]
    own_hidden = hidden_pair[0]
    stacked = jnp.concatenate([own_fields, velocity[None, :]], axis=0)
    advanced = advance(extended(stacked, "tile", 1, 1), growth)
    grad_out, grad_hidden, other_out, other_hidden, fresh_fields = training(
        features,
        own_hidden.astype(jnp.bfloat16),
        own_out.astype(jnp.bfloat16),
        own_fields,
        own_out,
        own_hidden,
        advanced.astype(jnp.bfloat16),
    )
    grad_out, grad_hidden, other_out, other_hidden = (
        v.astype(jnp.float32) for v in (grad_out, grad_hidden, other_out, other_hidden)
    )
    out_next = jnp.where(
        solver_side,
        momentum_decay * own_out + grad_out,
        own_out - step_size * (momentum_decay * other_out + grad_out),
    )
    hidden_next = jnp.where(
        solver_side,
        momentum_decay * own_hidden + other_hidden,
        own_hidden - step_size * (momentum_decay * other_hidden + grad_hidden),
    )
    next_batch = jnp.take(fresh_fields, assignment, axis=0).astype(jnp.float32)
    fields_next = jnp.where(solver_side, advanced, next_batch)
    return (fields_next[None], out_next[None], hidden_next[None])


def solution(mesh):
    return jax.shard_map(
        body,
        mesh=mesh,
        in_specs=(
            P("role", None, "tile"),
            P("tile"),
            P("tile"),
            P(),
            P(),
            P("role", None, "tile"),
            P("role", None, "tile", None),
        ),
        out_specs=(P("role", None, "tile"), P("role", None, "tile"), P("role", None, "tile", None)),
        check_vma=False,
    )
```
